128 devices in a mesh: row: 16 (over y, x), col: 8 (over z, core).
Axes of the slice: x: 4, y: 4, z: 4, core: 2. Of those that a mesh axis runs over, the one named last changes fastest.
Arguments:
- layer_input: bfloat16 [768, 8192], P('col', 'row'), may hold values from -6 to 6
- out_grad: bfloat16 [768, 8192], P('col', 'row'), may hold values from -6 to 6
- gate_weight: bfloat16 [8192, 28672], P('row', 'col'), may hold values from -0.0625 to 0.0625
- up_weight: bfloat16 [8192, 28672], P('row', 'col'), may hold values from -0.0625 to 0.0625
- down_weight: bfloat16 [28672, 8192], P('col', 'row'), may hold values from -0.03125 to 0.03125
Outputs:
- input_grad: bfloat16 [768, 8192], P('col', 'row')
- gate_grad: bfloat16 [8192, 28672], P('row', 'col')
- up_grad: bfloat16 [8192, 28672], P('row', 'col')
- down_grad: bfloat16 [28672, 8192], P('col', 'row')
The draws below stay inside these ranges and needn't reach their ends.
All inputs are finite; a program needn't handle non-finite values.
Results may differ from the reference program's by a relative error of at most 0.033.
Values may be sent and summed in bfloat16 or wider, within the bound.
A program may use at most 192 MiB of HBM per device.

```python
import jax
import jax.numpy as jnp
from jax import lax

D = 8192
FF = 28672
TOKENS = 768
N_ROW = 16


def levels(key, dims, pieces, smallest, top_value):
    level = 1.0
    for dim, blocks in pieces:
        draws = jax.random.uniform(jax.random.fold_in(jax.random.fold_in(key, 6), dim), (blocks,), jnp.float32, smallest / len(pieces), top_value / len(pieces))
        level = level * jnp.repeat(jnp.exp(draws), dims[dim] // blocks).reshape((-1,) + (1,) * (len(dims) - 1 - dim))
    return level


def scatter_about(key, shape, scale, reach, shards=(), kind=jnp.bfloat16):
    gain = levels(key, shape, shards, -0.22, 0.18) if shards else 1.0
    entries = jax.random.normal(key, shape, jnp.float32) * scale * gain
    return jnp.minimum(jnp.maximum(entries, -reach), reach).astype(kind)


def setup_inputs(seed: int = 0) -> dict:
    seeds = jax.random.split(jax.random.key(seed), 6)
    return {
        "layer_input": scatter_about(seeds[0], (TOKENS, D), 1.0, 6.0, ((0, 8), (1, 16))),
        "out_grad": scatter_about(seeds[1], (TOKENS, D), 1.0, 6.0, ((0, 8), (1, 16))),
        "gate_weight": scatter_about(seeds[2], (D, FF), D ** -0.5, 0.0625, ((0, 16), (1, 8))),
        "up_weight": scatter_about(seeds[3], (D, FF), D ** -0.5, 0.0625, ((0, 16), (1, 8))),
        "down_weight": scatter_about(seeds[4], (FF, D), FF ** -0.5, 0.03125, ((0, 8), (1, 16))),
    }


def block_sum(left, right, blocks):
    count = left.shape[0]
    width = left.shape[1] // blocks
    left_blocks = left.reshape(count, blocks, width).transpose(1, 0, 2)
    right_blocks = right.reshape(blocks, width, right.shape[1])

    def accumulate(total, pair):
        term = jnp.dot(pair[0], pair[1], preferred_element_type=jnp.float32).astype(jnp.bfloat16)
        term = lax.optimization_barrier(term)
        return total + term.astype(jnp.float32), None

    start = jnp.zeros((count, right.shape[1]), jnp.float32)
    total, unused = lax.scan(accumulate, start, (left_blocks, right_blocks))
    return total


def reference(layer_input, out_grad, gate_weight, up_weight, down_weight):
    gate = block_sum(layer_input, gate_weight, N_ROW)
    up = block_sum(layer_input, up_weight, N_ROW)
    hidden_grad = block_sum(out_grad, down_weight.T, N_ROW)
    sigma = jax.nn.sigmoid(gate)
    swish = gate * sigma
    hidden = (swish * up).astype(jnp.bfloat16)
    up_delta = (hidden_grad * swish).astype(jnp.bfloat16)
    gate_delta = (hidden_grad * up * sigma * (1.0 + gate * (1.0 - sigma))).astype(jnp.bfloat16)
    factor = 1.0 / (TOKENS ** 0.5)
    down_grad = (jnp.dot(hidden.T, out_grad, preferred_element_type=jnp.float32) * factor).astype(jnp.bfloat16)
    gate_grad = (jnp.dot(layer_input.T, gate_delta, preferred_element_type=jnp.float32) * factor).astype(jnp.bfloat16)
    up_grad = (jnp.dot(layer_input.T, up_delta, preferred_element_type=jnp.float32) * factor).astype(jnp.bfloat16)
    input_grad = jnp.dot(gate_delta, gate_weight.T, preferred_element_type=jnp.float32)
    input_grad = input_grad + jnp.dot(up_delta, up_weight.T, preferred_element_type=jnp.float32)
    return input_grad.astype(jnp.bfloat16), gate_grad, up_grad, down_grad
```

```python
import jax
import jax.numpy as jnp
from jax import lax
from jax.experimental import pallas as pl
from jax.experimental.pallas import tpu as pltpu
from jax.sharding import PartitionSpec as P

MESH = pl.DeviceIdType.MESH
BF = jnp.bfloat16
F32 = jnp.float32
NT = (((1,), (1,)), ((), ()))
TN = (((0,), (0,)), ((), ()))
GROUPS = 4
ROWS = 192
HALF = 96
SIDE = 4
BLOCK = 512
SLOTS = 12
LAG = 2


def stream_kernel(
    x_hbm, dy_hbm, wg_hbm, wu_hbm, wd_hbm,
    out_ref, g_hbm, xo_hbm,
    wg, wu, wd, xb, part, r1, r2, r3, r4, full, acc, stage, landed,
    w_sem, x_sem, xs_sem, xr_sem, ssem, rsem, is_sem, ir_sem, g_sem, xo_sem,
):
    blocks = wg.shape[1] // BLOCK
    units = GROUPS * blocks
    row = lax.axis_index("row")
    col = lax.axis_index("col")
    y, x = row // SIDE, lax.rem(row, SIDE)
    z, core = col // 2, lax.rem(col, 2)

    def add(a, n):
        return lax.rem(a + n, 4)

    def weight_copies(j):
        cols = pl.ds(pl.multiple_of(j * BLOCK, BLOCK), BLOCK)
        return (
            pltpu.make_async_copy(wg_hbm.at[:, cols], wg.at[:, cols], w_sem.at[0, j]),
            pltpu.make_async_copy(wu_hbm.at[:, cols], wu.at[:, cols], w_sem.at[1, j]),
            pltpu.make_async_copy(wd_hbm.at[cols, :], wd.at[cols, :], w_sem.at[2, j]),
        )

    own = (
        pltpu.make_async_copy(x_hbm, xb.at[col, 0], x_sem.at[0]),
        pltpu.make_async_copy(dy_hbm, xb.at[col, 1], x_sem.at[1]),
    )
    for c in own:
        c.start()

    @pl.loop(0, blocks)
    def _(j):
        for c in weight_copies(j):
            c.start()

    partners = [(z, 1 - core)] + [(add(z, 4 - d), k) for d in (1, 2, 3) for k in (0, 1)]
    around = [(y, add(x, 1)), (y, add(x, 3)), (add(y, 1), x), (add(y, 3), x)]
    barrier = pltpu.get_barrier_semaphore()
    for pz, pk in partners:
        pl.semaphore_signal(barrier, inc=1, device_id=(row, pz * 2 + pk), device_id_type=MESH)
    for py, px in around:
        pl.semaphore_signal(barrier, inc=1, device_id=(py * SIDE + px, col), device_id_type=MESH)
    pl.semaphore_wait(barrier, len(partners) + len(around))

    for c in own:
        c.wait()

    def shard_copy(n, source):
        pz, pk = partners[n]
        return pltpu.make_async_remote_copy(
            src_ref=xb.at[col], dst_ref=xb.at[source], send_sem=xs_sem.at[n], recv_sem=xr_sem.at[source],
            device_id=(row, pz * 2 + pk), device_id_type=MESH,
        )

    for n in range(len(partners)):
        shard_copy(n, col).start()
    shard_copy(0, z * 2 + 1 - core).wait_recv()

    def token_copy(s):
        group = add(z, s)
        return pltpu.make_async_copy(xb.at[pl.ds(group * 2, 2)], xo_hbm.at[s], xo_sem.at[s])

    def grad_copy(u):
        return pltpu.make_async_copy(full.at[u], g_hbm.at[u], g_sem.at[u])

    def term_copy(s, k):
        return pltpu.make_async_remote_copy(
            src_ref=stage.at[s, k], dst_ref=landed.at[col], send_sem=is_sem.at[s, k], recv_sem=ir_sem.at[col],
            device_id=(row, add(z, s) * 2 + k), device_id_type=MESH,
        )

    @pl.loop(0, units + 8 * LAG)
    def _(t):
        odd = lax.rem(t, 2)
        i1 = jnp.where(odd == 0, x, y)
        i2 = jnp.where(odd == 0, y, x)

        def device(d1, d2):
            a, b = add(i1, d1), add(i2, d2)
            ny, nx = jnp.where(odd == 0, b, a), jnp.where(odd == 0, a, b)
            return (ny * SIDE + nx, col)

        up1, down1, up2, down2 = device(1, 0), device(3, 0), device(0, 1), device(0, 3)
        n1, p1, f1 = add(i1, 1), add(i1, 3), add(i1, 2)
        n2, p2, f2 = add(i2, 1), add(i2, 3), add(i2, 2)

        def send(u, slot, m):
            src, dst, target = {
                0: (lambda: part.at[slot, f1, pl.ds(0, 2)], lambda: r1.at[slot, 0], up1),
                1: (lambda: part.at[slot, f1, pl.ds(2, 2)], lambda: r1.at[slot, 1], down1),
                2: (lambda: part.at[slot, n1], lambda: r2.at[slot, 0], up1),
                3: (lambda: part.at[slot, p1], lambda: r2.at[slot, 1], down1),
                4: (lambda: part.at[slot, i1, f2, pl.ds(0, 5)], lambda: r3.at[slot, pl.ds(0, 5)], up2),
                5: (lambda: part.at[slot, i1, f2, pl.ds(5, 4)], lambda: r3.at[slot, pl.ds(5, 4)], down2),
                6: (lambda: part.at[slot, i1, n2], lambda: r4.at[slot, 0], up2),
                7: (lambda: part.at[slot, i1, p2], lambda: r4.at[slot, 1], down2),
                8: (lambda: full.at[u, i1, i2], lambda: full.at[u, i1, i2], up2),
                9: (lambda: full.at[u, i1, i2], lambda: full.at[u, i1, i2], down2),
                10: (lambda: full.at[u, i1, p2, pl.ds(0, 5)], lambda: full.at[u, i1, p2, pl.ds(0, 5)], up2),
                11: (lambda: full.at[u, i1, n2, pl.ds(5, 4)], lambda: full.at[u, i1, n2, pl.ds(5, 4)], down2),
                12: (lambda: full.at[u, i1], lambda: full.at[u, i1], up1),
                13: (lambda: full.at[u, i1], lambda: full.at[u, i1], down1),
                14: (lambda: full.at[u, p1, pl.ds(0, 2)], lambda: full.at[u, p1, pl.ds(0, 2)], up1),
                15: (lambda: full.at[u, n1, pl.ds(2, 2)], lambda: full.at[u, n1, pl.ds(2, 2)], down1),
            }[m]
            return pltpu.make_async_remote_copy(
                src_ref=src(), dst_ref=dst(), send_sem=ssem.at[slot, m], recv_sem=rsem.at[slot, m],
                device_id=target, device_id_type=MESH,
            )

        def at_stage(k):
            u = t - k * LAG

            def run(body):
                @pl.when(jnp.logical_and(u >= 0, u < units))
                def _():
                    body(u, lax.rem(u, SLOTS))
            return run

        @at_stage(7)
        def _(u, slot):
            send(u, slot, 12).wait()
            send(u, slot, 14).start()
            send(u, slot, 13).wait()
            send(u, slot, 15).start()

        @at_stage(6)
        def _(u, slot):
            send(u, slot, 10).wait()
            send(u, slot, 11).wait()
            send(u, slot, 12).start()
            send(u, slot, 13).start()

        @at_stage(5)
        def _(u, slot):
            send(u, slot, 8).wait()
            send(u, slot, 10).start()
            send(u, slot, 9).wait()
            send(u, slot, 11).start()

        @at_stage(4)
        def _(u, slot):
            send(u, slot, 6).wait()
            send(u, slot, 7).wait()
            total = (
                part[slot, i1, i2].astype(F32) + r4[slot, 0].astype(F32) + r4[slot, 1].astype(F32)
            )
            gate, up, hidden_grad = total[0:3], total[3:6], total[6:9]
            sigma = 1.0 / (1.0 + jnp.exp(-gate))
            swish = gate * sigma
            full[u, i1, i2, 0:3] = (swish * up).astype(BF)
            full[u, i1, i2, 3:6] = (hidden_grad * up * sigma * (1.0 + gate * (1.0 - sigma))).astype(BF)
            full[u, i1, i2, 6:9] = (hidden_grad * swish).astype(BF)
            send(u, slot, 8).start()
            send(u, slot, 9).start()

        @at_stage(3)
        def _(u, slot):
            send(u, slot, 4).wait()
            part[slot, i1, n2, 0:5] = (part[slot, i1, n2, 0:5].astype(F32) + r3[slot, 0:5].astype(F32)).astype(BF)
            send(u, slot, 6).start()
            send(u, slot, 5).wait()
            part[slot, i1, p2, 5:9] = (part[slot, i1, p2, 5:9].astype(F32) + r3[slot, 5:9].astype(F32)).astype(BF)
            send(u, slot, 7).start()

        @at_stage(2)
        def _(u, slot):
            send(u, slot, 2).wait()
            send(u, slot, 3).wait()
            part[slot, i1] = (
                part[slot, i1].astype(F32) + r2[slot, 0].astype(F32) + r2[slot, 1].astype(F32)
            ).astype(BF)
            send(u, slot, 4).start()
            send(u, slot, 5).start()

        @at_stage(1)
        def _(u, slot):
            send(u, slot, 0).wait()
            part[slot, n1, 0:2] = (part[slot, n1, 0:2].astype(F32) + r1[slot, 0].astype(F32)).astype(BF)
            send(u, slot, 2).start()
            send(u, slot, 1).wait()
            part[slot, p1, 2:4] = (part[slot, p1, 2:4].astype(F32) + r1[slot, 1].astype(F32)).astype(BF)
            send(u, slot, 3).start()

        @at_stage(0)
        def _(u, slot):
            s, j = u // blocks, lax.rem(u, blocks)
            group = add(z, s)

            @pl.when(s == 0)
            def _():
                for c in weight_copies(j):
                    c.wait()

            @pl.when(jnp.logical_and(s > 0, j == 0))
            def _():
                for k in (0, 1):
                    shard_copy(1, group * 2 + k).wait_recv()

            @pl.when(j == 0)
            def _():
                token_copy(s).start()

            cols = pl.ds(pl.multiple_of(j * BLOCK, BLOCK), BLOCK)
            for arr in range(3):
                left = xb[pl.ds(group * 2, 2), arr // 2].reshape(ROWS, BLOCK)
                if arr == 0:
                    term = jnp.dot(left, wg[:, cols], preferred_element_type=F32)
                elif arr == 1:
                    term = jnp.dot(left, wu[:, cols], preferred_element_type=F32)
                else:
                    term = lax.dot_general(left, wd[cols, :], NT, preferred_element_type=F32)
                term = term.astype(BF)
                for a in range(4):
                    part[slot, a, :, 3 * arr : 3 * arr + 3] = term[:, 128 * a : 128 * a + 128].reshape(4, 3, 16, 128)
            send(u, slot, 0).start()
            send(u, slot, 1).start()

        @at_stage(8)
        def _(u, slot):
            s, j = u // blocks, lax.rem(u, blocks)
            send(u, slot, 14).wait()
            send(u, slot, 15).wait()
            grad_copy(u).start()

            @pl.when(j == 0)
            def _():
                acc[...] = jnp.zeros_like(acc)

            cols = pl.ds(pl.multiple_of(j * BLOCK, BLOCK), BLOCK)
            total = acc[...]
            for arr, weight in ((1, wg), (2, wu)):
                left = jnp.concatenate(
                    [full[u, a, :, 3 * arr : 3 * arr + 3].reshape(ROWS, 128) for a in range(4)], axis=1
                )
                total = total + lax.dot_general(left, weight[:, cols], NT, preferred_element_type=F32)
            acc[...] = total

            @pl.when(j == blocks - 1)
            def _():
                for k in (0, 1):
                    mine = jnp.logical_and(s == 0, core == k)

                    @pl.when(mine)
                    def _():
                        landed[col] = acc[HALF * k : HALF * (k + 1)].astype(BF)

                    @pl.when(jnp.logical_not(mine))
                    def _():
                        stage[s, k] = acc[HALF * k : HALF * (k + 1)].astype(BF)
                        term_copy(s, k).start()

    total = landed[col].astype(F32)
    for pz, pk in partners:
        source = pz * 2 + pk
        pltpu.make_async_remote_copy(
            src_ref=stage.at[0, 0], dst_ref=landed.at[source], send_sem=is_sem.at[0, 0], recv_sem=ir_sem.at[source],
            device_id=(row, source), device_id_type=MESH,
        ).wait_recv()
        total = total + landed[source].astype(F32)
    out_ref[...] = total.astype(BF)

    for n in range(len(partners)):
        shard_copy(n, col).wait_send()
    for s in range(GROUPS):
        token_copy(s).wait()
        for k in (0, 1):
            @pl.when(jnp.logical_not(jnp.logical_and(s == 0, core == k)))
            def _():
                term_copy(s, k).wait_send()

    @pl.loop(0, units)
    def _(u):
        grad_copy(u).wait()


def weight_kernel(factor, g_ref, x_ref, gate_ref, up_ref, down_ref, xt, dy):
    tokens = GROUPS * ROWS

    @pl.when(pl.program_id(0) == 0)
    def _():
        xt[...] = x_ref[:, :, 0].reshape(tokens, BLOCK).T
        dy[...] = x_ref[:, :, 1].reshape(tokens, BLOCK)

    def gathered(arr):
        return jnp.concatenate(
            [g_ref[:, 0, a, :, 3 * arr : 3 * arr + 3].reshape(tokens, 128) for a in range(4)], axis=1
        )

    gate_ref[...] = (jnp.dot(xt[...], gathered(1), preferred_element_type=F32) * factor).astype(BF)
    up_ref[...] = (jnp.dot(xt[...], gathered(2), preferred_element_type=F32) * factor).astype(BF)
    down_ref[...] = (lax.dot_general(gathered(0), dy[...], TN, preferred_element_type=F32) * factor).astype(BF)


def local(layer_input, out_grad, gate_weight, up_weight, down_weight):
    depth, width = gate_weight.shape
    blocks = width // BLOCK
    units = GROUPS * blocks
    any_spec = pl.BlockSpec(memory_space=pl.ANY)
    tile = (16, 128)
    input_grad, gathered, tokens = pl.pallas_call(
        stream_kernel,
        out_shape=(
            jax.ShapeDtypeStruct((HALF, depth), BF),
            jax.ShapeDtypeStruct((units, 4, 4, 9) + tile, BF),
            jax.ShapeDtypeStruct((GROUPS, 2, 2, HALF, depth), BF),
        ),
        in_specs=[any_spec] * 5,
        out_specs=(pl.BlockSpec(memory_space=pltpu.VMEM), any_spec, any_spec),
        scratch_shapes=[
            pltpu.VMEM((depth, width), BF),
            pltpu.VMEM((depth, width), BF),
            pltpu.VMEM((width, depth), BF),
            pltpu.VMEM((8, 2, HALF, depth), BF),
            pltpu.VMEM((SLOTS, 4, 4, 9) + tile, BF),
            pltpu.VMEM((SLOTS, 2, 2, 9) + tile, BF),
            pltpu.VMEM((SLOTS, 2, 4, 9) + tile, BF),
            pltpu.VMEM((SLOTS, 9) + tile, BF),
            pltpu.VMEM((SLOTS, 2, 9) + tile, BF),
            pltpu.VMEM((units, 4, 4, 9) + tile, BF),
            pltpu.VMEM((ROWS, depth), F32),
            pltpu.VMEM((GROUPS, 2, HALF, depth), BF),
            pltpu.VMEM((8, HALF, depth), BF),
            pltpu.SemaphoreType.DMA((3, blocks)),
            pltpu.SemaphoreType.DMA((2,)),
            pltpu.SemaphoreType.DMA((7,)),
            pltpu.SemaphoreType.DMA((8,)),
            pltpu.SemaphoreType.DMA((SLOTS, 16)),
            pltpu.SemaphoreType.DMA((SLOTS, 16)),
            pltpu.SemaphoreType.DMA((GROUPS, 2)),
            pltpu.SemaphoreType.DMA((8,)),
            pltpu.SemaphoreType.DMA((units,)),
            pltpu.SemaphoreType.DMA((GROUPS,)),
        ],
        compiler_params=pltpu.CompilerParams(
            collective_id=0, has_side_effects=True, vmem_limit_bytes=60 * 2**20
        ),
        name="stream",
    )(layer_input, out_grad, gate_weight, up_weight, down_weight)
    factor = 1.0 / (GROUPS * ROWS) ** 0.5
    gate_grad, up_grad, down_grad = pl.pallas_call(
        lambda *refs: weight_kernel(factor, *refs),
        grid=(blocks,),
        out_shape=(
            jax.ShapeDtypeStruct((depth, width), BF),
            jax.ShapeDtypeStruct((depth, width), BF),
            jax.ShapeDtypeStruct((width, depth), BF),
        ),
        in_specs=[
            pl.BlockSpec((GROUPS, 1, 4, 4, 9) + tile, lambda j: (0, j, 0, 0, 0, 0, 0)),
            pl.BlockSpec((GROUPS, 2, 2, HALF, depth), lambda j: (0, 0, 0, 0, 0)),
        ],
        out_specs=(
            pl.BlockSpec((depth, BLOCK), lambda j: (0, j)),
            pl.BlockSpec((depth, BLOCK), lambda j: (0, j)),
            pl.BlockSpec((BLOCK, depth), lambda j: (j, 0)),
        ),
        scratch_shapes=[
            pltpu.VMEM((depth, GROUPS * ROWS), BF),
            pltpu.VMEM((GROUPS * ROWS, depth), BF),
        ],
        compiler_params=pltpu.CompilerParams(vmem_limit_bytes=40 * 2**20),
        name="weight_grads",
    )(gathered.reshape((GROUPS, blocks, 4, 4, 9) + tile), tokens)
    return (input_grad, gate_grad, up_grad, down_grad)


def solution(mesh):
    placed = (P("col", "row"), P("col", "row"), P("row", "col"), P("row", "col"), P("col", "row"))
    return jax.shard_map(
        local,
        mesh=mesh,
        in_specs=placed,
        out_specs=(P("col", "row"), P("row", "col"), P("row", "col"), P("col", "row")),
        check_vma=False,
    )
```

```python
import functools

import jax
import jax.numpy as jnp
from jax import lax
from jax.experimental import pallas as pl
from jax.experimental.pallas import tpu as pltpu
from jax.sharding import PartitionSpec as P

MESH = pl.DeviceIdType.MESH
BF = jnp.bfloat16
F32 = jnp.float32
NT = (((1,), (1,)), ((), ()))
TN = (((0,), (0,)), ((), ()))
GROUPS = 4
ROWS = 192
HALF = 96
SIDE = 4
BLOCK = 512
SLOTS = 14
STAGES = (0, 2, 4, 6, 8, 10, 12, 14, 16)


def stream_kernel(
    factor, x_hbm, dy_hbm, wg_hbm, wu_hbm, wd_hbm,
    out_ref, wg, wu, wd,
    xb, xt, part, r1, r2, r3, r4, full, acc, stage, landed,
    w_sem, x_sem, xs_sem, xr_sem, ssem, rsem, is_sem, ir_sem,
):
    blocks = wg.shape[1] // BLOCK
    units = GROUPS * blocks
    row = lax.axis_index("row")
    col = lax.axis_index("col")
    y, x = row // SIDE, lax.rem(row, SIDE)
    z, core = col // 2, lax.rem(col, 2)

    def add(a, n):
        return lax.rem(a + n, 4)

    def weight_copies(j):
        cols = pl.ds(pl.multiple_of(j * BLOCK, BLOCK), BLOCK)
        return (
            pltpu.make_async_copy(wg_hbm.at[:, cols], wg.at[:, cols], w_sem.at[0, j]),
            pltpu.make_async_copy(wu_hbm.at[:, cols], wu.at[:, cols], w_sem.at[1, j]),
            pltpu.make_async_copy(wd_hbm.at[cols, :], wd.at[cols, :], w_sem.at[2, j]),
        )

    own = (
        pltpu.make_async_copy(x_hbm, xb.at[col, 0], x_sem.at[0]),
        pltpu.make_async_copy(dy_hbm, xb.at[col, 1], x_sem.at[1]),
    )
    for c in weight_copies(0) + own + weight_copies(1):
        c.start()

    partners = [(z, 1 - core)] + [(add(z, 4 - d), k) for d in (1, 2, 3) for k in (0, 1)]
    around = [(y, add(x, 1)), (y, add(x, 3)), (add(y, 1), x), (add(y, 3), x)]
    barrier = pltpu.get_barrier_semaphore()
    for pz, pk in partners:
        pl.semaphore_signal(barrier, inc=1, device_id=(row, pz * 2 + pk), device_id_type=MESH)
    for py, px in around:
        pl.semaphore_signal(barrier, inc=1, device_id=(py * SIDE + px, col), device_id_type=MESH)
    pl.semaphore_wait(barrier, len(partners) + len(around))

    def shard_copies(n, source):
        pz, pk = partners[n]
        return [
            pltpu.make_async_remote_copy(
                src_ref=ref, dst_ref=xb.at[source, h], send_sem=xs_sem.at[n, h], recv_sem=xr_sem.at[source, h],
                device_id=(row, pz * 2 + pk), device_id_type=MESH,
            )
            for h, ref in enumerate((x_hbm, dy_hbm))
        ]

    for n in range(len(partners)):
        for c in shard_copies(n, col):
            c.start()
    for c in own:
        c.wait()
    for c in shard_copies(0, z * 2 + 1 - core):
        c.wait_recv()

    def term_copy(s, k):
        return pltpu.make_async_remote_copy(
            src_ref=stage.at[s, k], dst_ref=landed.at[col], send_sem=is_sem.at[s, k], recv_sem=ir_sem.at[col],
            device_id=(row, add(z, s) * 2 + k), device_id_type=MESH,
        )

    @pl.loop(0, units + STAGES[-1])
    def _(t):
        def send(u, slot, m):
            even = lax.rem(u, 2) == 0
            i1, i2 = jnp.where(even, x, y), jnp.where(even, y, x)

            def device(d1, d2):
                a, b = add(i1, d1), add(i2, d2)
                return (jnp.where(even, b, a) * SIDE + jnp.where(even, a, b), col)

            up1, down1, up2, down2 = device(1, 0), device(3, 0), device(0, 1), device(0, 3)
            n1, p1, f1 = add(i1, 1), add(i1, 3), add(i1, 2)
            n2, p2, f2 = add(i2, 1), add(i2, 3), add(i2, 2)
            src, dst, target = {
                0: (lambda: part.at[slot, f1, pl.ds(0, 2)], lambda: r1.at[slot, 0], up1),
                1: (lambda: part.at[slot, f1, pl.ds(2, 2)], lambda: r1.at[slot, 1], down1),
                2: (lambda: part.at[slot, n1, pl.ds(0, 2)], lambda: r2.at[slot, 0, pl.ds(0, 2)], up1),
                3: (lambda: part.at[slot, p1, pl.ds(2, 2)], lambda: r2.at[slot, 1, pl.ds(2, 2)], down1),
                4: (lambda: part.at[slot, i1, f2, pl.ds(0, 5)], lambda: r3.at[slot, pl.ds(0, 5)], up2),
                5: (lambda: part.at[slot, i1, f2, pl.ds(5, 4)], lambda: r3.at[slot, pl.ds(5, 4)], down2),
                6: (lambda: part.at[slot, i1, n2], lambda: r4.at[slot, 0], up2),
                7: (lambda: part.at[slot, i1, p2], lambda: r4.at[slot, 1], down2),
                8: (lambda: full.at[u, i1, i2], lambda: full.at[u, i1, i2], up2),
                9: (lambda: full.at[u, i1, i2], lambda: full.at[u, i1, i2], down2),
                10: (lambda: full.at[u, i1, p2, pl.ds(0, 5)], lambda: full.at[u, i1, p2, pl.ds(0, 5)], up2),
                11: (lambda: full.at[u, i1, n2, pl.ds(5, 4)], lambda: full.at[u, i1, n2, pl.ds(5, 4)], down2),
                12: (lambda: full.at[u, i1, pl.ds(0, 2)], lambda: full.at[u, i1, pl.ds(0, 2)], up1),
                13: (lambda: full.at[u, i1, pl.ds(2, 2)], lambda: full.at[u, i1, pl.ds(2, 2)], down1),
                14: (lambda: full.at[u, p1, pl.ds(0, 2)], lambda: full.at[u, p1, pl.ds(0, 2)], up1),
                15: (lambda: full.at[u, n1, pl.ds(2, 2)], lambda: full.at[u, n1, pl.ds(2, 2)], down1),
                16: (lambda: part.at[slot, n1, pl.ds(2, 2)], lambda: r2.at[slot, 0, pl.ds(2, 2)], up1),
                17: (lambda: part.at[slot, p1, pl.ds(0, 2)], lambda: r2.at[slot, 1, pl.ds(0, 2)], down1),
                18: (lambda: full.at[u, i1, pl.ds(2, 2)], lambda: full.at[u, i1, pl.ds(2, 2)], up1),
                19: (lambda: full.at[u, i1, pl.ds(0, 2)], lambda: full.at[u, i1, pl.ds(0, 2)], down1),
            }[m]
            return pltpu.make_async_remote_copy(
                src_ref=src(), dst_ref=dst(), send_sem=ssem.at[slot, m], recv_sem=rsem.at[slot, m],
                device_id=target, device_id_type=MESH,
            )

        def at_stage(k):
            u = t - STAGES[k]

            def run(body):
                @pl.when(jnp.logical_and(u >= 0, u < units))
                def _():
                    even = lax.rem(u, 2) == 0
                    i1, i2 = jnp.where(even, x, y), jnp.where(even, y, x)
                    body(u, lax.rem(u, SLOTS), i1, i2)
            return run

        @at_stage(7)
        def _(u, slot, i1, i2):
            send(u, slot, 12).wait()
            send(u, slot, 14).start()
            send(u, slot, 13).wait()
            send(u, slot, 15).start()

        @at_stage(6)
        def _(u, slot, i1, i2):
            send(u, slot, 10).wait()
            send(u, slot, 11).wait()
            for m in (12, 13, 18, 19):
                send(u, slot, m).start()

        @at_stage(5)
        def _(u, slot, i1, i2):
            send(u, slot, 8).wait()
            send(u, slot, 10).start()
            send(u, slot, 9).wait()
            send(u, slot, 11).start()

        @at_stage(4)
        def _(u, slot, i1, i2):
            send(u, slot, 6).wait()
            send(u, slot, 7).wait()
            total = (
                part[slot, i1, i2].astype(F32) + r4[slot, 0].astype(F32) + r4[slot, 1].astype(F32)
            )
            gate, up, hidden_grad = total[0:3], total[3:6], total[6:9]
            sigma = 1.0 / (1.0 + jnp.exp(-gate))
            swish = gate * sigma
            full[u, i1, i2, 0:3] = (swish * up).astype(BF)
            full[u, i1, i2, 3:6] = (hidden_grad * up * sigma * (1.0 + gate * (1.0 - sigma))).astype(BF)
            full[u, i1, i2, 6:9] = (hidden_grad * swish).astype(BF)
            send(u, slot, 8).start()
            send(u, slot, 9).start()

        @at_stage(3)
        def _(u, slot, i1, i2):
            send(u, slot, 4).wait()
            part[slot, i1, add(i2, 1), 0:5] = (part[slot, i1, add(i2, 1), 0:5].astype(F32) + r3[slot, 0:5].astype(F32)).astype(BF)
            send(u, slot, 6).start()
            send(u, slot, 5).wait()
            part[slot, i1, add(i2, 3), 5:9] = (part[slot, i1, add(i2, 3), 5:9].astype(F32) + r3[slot, 5:9].astype(F32)).astype(BF)
            send(u, slot, 7).start()

        @at_stage(2)
        def _(u, slot, i1, i2):
            for m in (16, 17, 2, 3):
                send(u, slot, m).wait()
            part[slot, i1] = (
                part[slot, i1].astype(F32) + r2[slot, 0].astype(F32) + r2[slot, 1].astype(F32)
            ).astype(BF)
            send(u, slot, 4).start()
            send(u, slot, 5).start()

        @at_stage(1)
        def _(u, slot, i1, i2):
            send(u, slot, 0).wait()
            part[slot, add(i1, 1), 0:2] = (part[slot, add(i1, 1), 0:2].astype(F32) + r1[slot, 0].astype(F32)).astype(BF)
            send(u, slot, 2).start()
            send(u, slot, 1).wait()
            part[slot, add(i1, 3), 2:4] = (part[slot, add(i1, 3), 2:4].astype(F32) + r1[slot, 1].astype(F32)).astype(BF)
            send(u, slot, 3).start()

        @at_stage(0)
        def _(u, slot, i1, i2):
            s, j = u // blocks, lax.rem(u, blocks)
            group = add(z, s)

            @pl.when(s == 0)
            def _():
                for c in weight_copies(j):
                    c.wait()

                @pl.when(j + 2 < blocks)
                def _():
                    for c in weight_copies(j + 2):
                        c.start()

            @pl.when(jnp.logical_and(s > 0, j == 0))
            def _():
                for k in (0, 1):
                    for c in shard_copies(1, group * 2 + k):
                        c.wait_recv()

            @pl.when(jnp.logical_and(s == GROUPS - 1, j == 1))
            def _():
                for n in range(GROUPS):
                    xt[n] = xb[pl.ds(add(z, n) * 2, 2), 0].reshape(ROWS, BLOCK).T

            cols = pl.ds(pl.multiple_of(j * BLOCK, BLOCK), BLOCK)
            for arr in range(3):
                left = xb[pl.ds(group * 2, 2), arr // 2].reshape(ROWS, BLOCK)
                if arr == 0:
                    term = jnp.dot(left, wg[:, cols], preferred_element_type=F32)
                elif arr == 1:
                    term = jnp.dot(left, wu[:, cols], preferred_element_type=F32)
                else:
                    term = lax.dot_general(left, wd[cols, :], NT, preferred_element_type=F32)
                term = term.astype(BF)
                for a in range(4):
                    part[slot, a, :, 3 * arr : 3 * arr + 3] = term[:, 128 * a : 128 * a + 128].reshape(4, 3, 16, 128)
            for m in (0, 1, 16, 17):
                send(u, slot, m).start()

        @at_stage(8)
        def _(u, slot, i1, i2):
            s, j = u // blocks, lax.rem(u, blocks)
            for m in (18, 19, 14, 15):
                send(u, slot, m).wait()

            @pl.when(j == 0)
            def _():
                acc[...] = jnp.zeros_like(acc)

            cols = pl.ds(pl.multiple_of(j * BLOCK, BLOCK), BLOCK)
            total = acc[...]
            for arr, weight in ((1, wg), (2, wu)):
                left = jnp.concatenate(
                    [full[u, a, :, 3 * arr : 3 * arr + 3].reshape(ROWS, 128) for a in range(4)], axis=1
                )
                total = total + lax.dot_general(left, weight[:, cols], NT, preferred_element_type=F32)
            acc[...] = total

            @pl.when(j == blocks - 1)
            def _():
                for k in (0, 1):
                    mine = jnp.logical_and(s == 0, core == k)

                    @pl.when(mine)
                    def _():
                        landed[col] = acc[HALF * k : HALF * (k + 1)].astype(BF)

                    @pl.when(jnp.logical_not(mine))
                    def _():
                        stage[s, k] = acc[HALF * k : HALF * (k + 1)].astype(BF)
                        term_copy(s, k).start()

            @pl.when(s == GROUPS - 1)
            def _():
                def gathered(arr, n):
                    return jnp.concatenate(
                        [full[n * blocks + j, a, :, 3 * arr : 3 * arr + 3].reshape(ROWS, 128) for a in range(4)],
                        axis=1,
                    )

                for arr, grad in ((1, wg), (2, wu)):
                    total = jnp.dot(xt[0], gathered(arr, 0), preferred_element_type=F32)
                    for n in range(1, GROUPS):
                        total = total + jnp.dot(xt[n], gathered(arr, n), preferred_element_type=F32)
                    grad[:, cols] = (total * factor).astype(BF)
                hidden = jnp.concatenate([gathered(0, n) for n in range(GROUPS)], axis=0)
                right = jnp.concatenate(
                    [xb[pl.ds(add(z, n) * 2, 2), 1].reshape(ROWS, BLOCK) for n in range(GROUPS)], axis=0
                )
                wd[cols, :] = (lax.dot_general(hidden, right, TN, preferred_element_type=F32) * factor).astype(BF)

    total = landed[col].astype(F32)
    for pz, pk in partners:
        source = pz * 2 + pk
        pltpu.make_async_remote_copy(
            src_ref=stage.at[0, 0], dst_ref=landed.at[source], send_sem=is_sem.at[0, 0], recv_sem=ir_sem.at[source],
            device_id=(row, source), device_id_type=MESH,
        ).wait_recv()
        total = total + landed[source].astype(F32)
    out_ref[...] = total.astype(BF)

    for n in range(len(partners)):
        for c in shard_copies(n, col):
            c.wait_send()
    for s in range(GROUPS):
        for k in (0, 1):
            @pl.when(jnp.logical_not(jnp.logical_and(s == 0, core == k)))
            def _():
                term_copy(s, k).wait_send()


def local(layer_input, out_grad, gate_weight, up_weight, down_weight):
    depth, width = gate_weight.shape
    blocks = width // BLOCK
    units = GROUPS * blocks
    any_spec = pl.BlockSpec(memory_space=pl.ANY)
    tile = (16, 128)
    return pl.pallas_call(
        functools.partial(stream_kernel, 1.0 / (GROUPS * ROWS) ** 0.5),
        out_shape=(
            pltpu.VMEM((HALF, depth), BF),
            pltpu.VMEM((depth, width), BF),
            pltpu.VMEM((depth, width), BF),
            pltpu.VMEM((width, depth), BF),
        ),
        in_specs=[any_spec] * 5,
        out_specs=(pl.BlockSpec(memory_space=pltpu.VMEM),) * 4,
        scratch_shapes=[
            pltpu.VMEM((8, 2, HALF, depth), BF),
            pltpu.VMEM((GROUPS, depth, ROWS), BF),
            pltpu.VMEM((SLOTS, 4, 4, 9) + tile, BF),
            pltpu.VMEM((SLOTS, 2, 2, 9) + tile, BF),
            pltpu.VMEM((SLOTS, 2, 4, 9) + tile, BF),
            pltpu.VMEM((SLOTS, 9) + tile, BF),
            pltpu.VMEM((SLOTS, 2, 9) + tile, BF),
            pltpu.VMEM((units, 4, 4, 9) + tile, BF),
            pltpu.VMEM((ROWS, depth), F32),
            pltpu.VMEM((GROUPS, 2, HALF, depth), BF),
            pltpu.VMEM((8, HALF, depth), BF),
            pltpu.SemaphoreType.DMA((3, blocks)),
            pltpu.SemaphoreType.DMA((2,)),
            pltpu.SemaphoreType.DMA((7, 2)),
            pltpu.SemaphoreType.DMA((8, 2)),
            pltpu.SemaphoreType.DMA((SLOTS, 20)),
            pltpu.SemaphoreType.DMA((SLOTS, 20)),
            pltpu.SemaphoreType.DMA((GROUPS, 2)),
            pltpu.SemaphoreType.DMA((8,)),
        ],
        compiler_params=pltpu.CompilerParams(
            collective_id=0, has_side_effects=True, vmem_limit_bytes=48 * 2**20
        ),
        name="stream",
    )(layer_input, out_grad, gate_weight, up_weight, down_weight)


def solution(mesh):
    placed = (P("col", "row"), P("col", "row"), P("row", "col"), P("row", "col"), P("col", "row"))
    return jax.shard_map(
        local,
        mesh=mesh,
        in_specs=placed,
        out_specs=(P("col", "row"), P("row", "col"), P("row", "col"), P("col", "row")),
        check_vma=False,
    )
```

```python
import functools

import jax
import jax.numpy as jnp
from jax import lax
from jax.experimental import pallas as pl
from jax.experimental.pallas import tpu as pltpu
from jax.sharding import PartitionSpec as P

MESH = pl.DeviceIdType.MESH
BF = jnp.bfloat16
F32 = jnp.float32
NT = (((1,), (1,)), ((), ()))
TN = (((0,), (0,)), ((), ()))
GROUPS = 4
ROWS = 192
HALF = 96
SIDE = 4
BLOCK = 512
SLOTS = 14
TAIL = 2
STAGES = (0, 2, 4, 6, 8, 10, 12, 14, 16)


def stream_kernel(
    factor, x_hbm, dy_hbm, wg_hbm, wu_hbm, wd_hbm,
    out_ref, wg, wu, wd,
    xb, xt, part, r1, r2, r3, r4, full, acc, stage, landed,
    w_sem, x_sem, xs_sem, xr_sem, ssem, rsem, is_sem, ir_sem,
):
    blocks = wg.shape[1] // BLOCK
    units = GROUPS * blocks
    row = lax.axis_index("row")
    col = lax.axis_index("col")
    y, x = row // SIDE, lax.rem(row, SIDE)
    z, core = col // 2, lax.rem(col, 2)

    def add(a, n):
        return lax.rem(a + n, 4)

    def group_and_block(u):
        v = u - 2 * blocks
        s = jnp.where(v < 0, jnp.where(u < blocks, 0, 2), 1 + 2 * lax.rem(jnp.maximum(v, 0), 2))
        return s, jnp.where(v < 0, lax.rem(u, blocks), jnp.maximum(v, 0) // 2)

    def unit_of(n, j):
        return (j, 2 * blocks + 2 * j, blocks + j, 2 * blocks + 1 + 2 * j)[n]

    def weight_copies(j):
        cols = pl.ds(pl.multiple_of(j * BLOCK, BLOCK), BLOCK)
        return (
            pltpu.make_async_copy(wg_hbm.at[:, cols], wg.at[:, cols], w_sem.at[0, j]),
            pltpu.make_async_copy(wu_hbm.at[:, cols], wu.at[:, cols], w_sem.at[1, j]),
            pltpu.make_async_copy(wd_hbm.at[cols, :], wd.at[cols, :], w_sem.at[2, j]),
        )

    own = (
        pltpu.make_async_copy(x_hbm, xb.at[col, 0], x_sem.at[0]),
        pltpu.make_async_copy(dy_hbm, xb.at[col, 1], x_sem.at[1]),
    )
    for c in weight_copies(0) + own + weight_copies(1):
        c.start()

    partners = [(z, 1 - core)] + [(add(z, 4 - d), k) for d in (1, 2, 3) for k in (0, 1)]
    around = [(y, add(x, 1)), (y, add(x, 3)), (add(y, 1), x), (add(y, 3), x)]
    barrier = pltpu.get_barrier_semaphore()
    for pz, pk in partners:
        pl.semaphore_signal(barrier, inc=1, device_id=(row, pz * 2 + pk), device_id_type=MESH)
    for py, px in around:
        pl.semaphore_signal(barrier, inc=1, device_id=(py * SIDE + px, col), device_id_type=MESH)
    pl.semaphore_wait(barrier, len(partners) + len(around))

    def shard_copies(n, source):
        pz, pk = partners[n]
        return [
            pltpu.make_async_remote_copy(
                src_ref=ref, dst_ref=xb.at[source, h], send_sem=xs_sem.at[n, h], recv_sem=xr_sem.at[source, h],
                device_id=(row, pz * 2 + pk), device_id_type=MESH,
            )
            for h, ref in enumerate((x_hbm, dy_hbm))
        ]

    for n in range(len(partners)):
        for c in shard_copies(n, col):
            c.start()
    for c in own:
        c.wait()
    for c in shard_copies(0, z * 2 + 1 - core):
        c.wait_recv()

    def term_copy(s, k):
        return pltpu.make_async_remote_copy(
            src_ref=stage.at[s, k], dst_ref=landed.at[col], send_sem=is_sem.at[s, k], recv_sem=ir_sem.at[col],
            device_id=(row, add(z, s) * 2 + k), device_id_type=MESH,
        )

    def weight_grads(j):
        cols = pl.ds(pl.multiple_of(j * BLOCK, BLOCK), BLOCK)

        def gathered(arr, n):
            return jnp.concatenate(
                [full[unit_of(n, j), a, :, 3 * arr : 3 * arr + 3].reshape(ROWS, 128) for a in range(4)],
                axis=1,
            )

        for arr, grad in ((1, wg), (2, wu)):
            total = jnp.dot(xt[0], gathered(arr, 0), preferred_element_type=F32)
            for n in range(1, GROUPS):
                total = total + jnp.dot(xt[n], gathered(arr, n), preferred_element_type=F32)
            grad[:, cols] = (total * factor).astype(BF)
        hidden = jnp.concatenate([gathered(0, n) for n in range(GROUPS)], axis=0)
        right = jnp.concatenate(
            [xb[pl.ds(add(z, n) * 2, 2), 1].reshape(ROWS, BLOCK) for n in range(GROUPS)], axis=0
        )
        wd[cols, :] = (lax.dot_general(hidden, right, TN, preferred_element_type=F32) * factor).astype(BF)

    @pl.loop(0, units + STAGES[-1])
    def _(t):
        def send(u, slot, m):
            even = lax.rem(u, 2) == 0
            i1, i2 = jnp.where(even, x, y), jnp.where(even, y, x)

            def device(d1, d2):
                a, b = add(i1, d1), add(i2, d2)
                return (jnp.where(even, b, a) * SIDE + jnp.where(even, a, b), col)

            up1, down1, up2, down2 = device(1, 0), device(3, 0), device(0, 1), device(0, 3)
            n1, p1, f1 = add(i1, 1), add(i1, 3), add(i1, 2)
            n2, p2, f2 = add(i2, 1), add(i2, 3), add(i2, 2)
            src, dst, target = {
                0: (lambda: part.at[slot, f1, pl.ds(0, 2)], lambda: r1.at[slot, 0], up1),
                1: (lambda: part.at[slot, f1, pl.ds(2, 2)], lambda: r1.at[slot, 1], down1),
                2: (lambda: part.at[slot, n1, pl.ds(0, 2)], lambda: r2.at[slot, 0, pl.ds(0, 2)], up1),
                3: (lambda: part.at[slot, p1, pl.ds(2, 2)], lambda: r2.at[slot, 1, pl.ds(2, 2)], down1),
                4: (lambda: part.at[slot, i1, f2, pl.ds(0, 5)], lambda: r3.at[slot, pl.ds(0, 5)], up2),
                5: (lambda: part.at[slot, i1, f2, pl.ds(5, 4)], lambda: r3.at[slot, pl.ds(5, 4)], down2),
                6: (lambda: part.at[slot, i1, n2], lambda: r4.at[slot, 0], up2),
                7: (lambda: part.at[slot, i1, p2], lambda: r4.at[slot, 1], down2),
                8: (lambda: full.at[u, i1, i2], lambda: full.at[u, i1, i2], up2),
                9: (lambda: full.at[u, i1, i2], lambda: full.at[u, i1, i2], down2),
                10: (lambda: full.at[u, i1, p2, pl.ds(0, 5)], lambda: full.at[u, i1, p2, pl.ds(0, 5)], up2),
                11: (lambda: full.at[u, i1, n2, pl.ds(5, 4)], lambda: full.at[u, i1, n2, pl.ds(5, 4)], down2),
                12: (lambda: full.at[u, i1, pl.ds(0, 2)], lambda: full.at[u, i1, pl.ds(0, 2)], up1),
                13: (lambda: full.at[u, i1, pl.ds(2, 2)], lambda: full.at[u, i1, pl.ds(2, 2)], down1),
                14: (lambda: full.at[u, p1, pl.ds(0, 2)], lambda: full.at[u, p1, pl.ds(0, 2)], up1),
                15: (lambda: full.at[u, n1, pl.ds(2, 2)], lambda: full.at[u, n1, pl.ds(2, 2)], down1),
                16: (lambda: part.at[slot, n1, pl.ds(2, 2)], lambda: r2.at[slot, 0, pl.ds(2, 2)], up1),
                17: (lambda: part.at[slot, p1, pl.ds(0, 2)], lambda: r2.at[slot, 1, pl.ds(0, 2)], down1),
                18: (lambda: full.at[u, i1, pl.ds(2, 2)], lambda: full.at[u, i1, pl.ds(2, 2)], up1),
                19: (lambda: full.at[u, i1, pl.ds(0, 2)], lambda: full.at[u, i1, pl.ds(0, 2)], down1),
            }[m]
            return pltpu.make_async_remote_copy(
                src_ref=src(), dst_ref=dst(), send_sem=ssem.at[slot, m], recv_sem=rsem.at[slot, m],
                device_id=target, device_id_type=MESH,
            )

        def at_stage(k):
            u = t - STAGES[k]

            def run(body):
                @pl.when(jnp.logical_and(u >= 0, u < units))
                def _():
                    even = lax.rem(u, 2) == 0
                    i1, i2 = jnp.where(even, x, y), jnp.where(even, y, x)
                    body(u, lax.rem(u, SLOTS), i1, i2)
            return run

        @at_stage(7)
        def _(u, slot, i1, i2):
            send(u, slot, 12).wait()
            send(u, slot, 14).start()
            send(u, slot, 13).wait()
            send(u, slot, 15).start()

        @at_stage(6)
        def _(u, slot, i1, i2):
            send(u, slot, 10).wait()
            send(u, slot, 11).wait()
            for m in (12, 13, 18, 19):
                send(u, slot, m).start()

        @at_stage(5)
        def _(u, slot, i1, i2):
            send(u, slot, 8).wait()
            send(u, slot, 10).start()
            send(u, slot, 9).wait()
            send(u, slot, 11).start()

        @at_stage(4)
        def _(u, slot, i1, i2):
            send(u, slot, 6).wait()
            send(u, slot, 7).wait()
            total = (
                part[slot, i1, i2].astype(F32) + r4[slot, 0].astype(F32) + r4[slot, 1].astype(F32)
            )
            gate, up, hidden_grad = total[0:3], total[3:6], total[6:9]
            sigma = 1.0 / (1.0 + jnp.exp(-gate))
            swish = gate * sigma
            full[u, i1, i2, 0:3] = (swish * up).astype(BF)
            full[u, i1, i2, 3:6] = (hidden_grad * up * sigma * (1.0 + gate * (1.0 - sigma))).astype(BF)
            full[u, i1, i2, 6:9] = (hidden_grad * swish).astype(BF)
            send(u, slot, 8).start()
            send(u, slot, 9).start()

        @at_stage(3)
        def _(u, slot, i1, i2):
            send(u, slot, 4).wait()
            part[slot, i1, add(i2, 1), 0:5] = (part[slot, i1, add(i2, 1), 0:5].astype(F32) + r3[slot, 0:5].astype(F32)).astype(BF)
            send(u, slot, 6).start()
            send(u, slot, 5).wait()
            part[slot, i1, add(i2, 3), 5:9] = (part[slot, i1, add(i2, 3), 5:9].astype(F32) + r3[slot, 5:9].astype(F32)).astype(BF)
            send(u, slot, 7).start()

        @at_stage(2)
        def _(u, slot, i1, i2):
            for m in (16, 17, 2, 3):
                send(u, slot, m).wait()
            part[slot, i1] = (
                part[slot, i1].astype(F32) + r2[slot, 0].astype(F32) + r2[slot, 1].astype(F32)
            ).astype(BF)
            send(u, slot, 4).start()
            send(u, slot, 5).start()

        @at_stage(1)
        def _(u, slot, i1, i2):
            send(u, slot, 0).wait()
            part[slot, add(i1, 1), 0:2] = (part[slot, add(i1, 1), 0:2].astype(F32) + r1[slot, 0].astype(F32)).astype(BF)
            send(u, slot, 2).start()
            send(u, slot, 1).wait()
            part[slot, add(i1, 3), 2:4] = (part[slot, add(i1, 3), 2:4].astype(F32) + r1[slot, 1].astype(F32)).astype(BF)
            send(u, slot, 3).start()

        @at_stage(0)
        def _(u, slot, i1, i2):
            s, j = group_and_block(u)
            group = add(z, s)

            @pl.when(s == 0)
            def _():
                for c in weight_copies(j):
                    c.wait()

                @pl.when(j + 2 < blocks)
                def _():
                    for c in weight_copies(j + 2):
                        c.start()

            @pl.when(jnp.logical_and(s > 0, j == 0))
            def _():
                for k in (0, 1):
                    for c in shard_copies(1, group * 2 + k):
                        c.wait_recv()

            @pl.when(jnp.logical_and(s == GROUPS - 1, j == 1))
            def _():
                for n in range(GROUPS):
                    xt[n] = xb[pl.ds(add(z, n) * 2, 2), 0].reshape(ROWS, BLOCK).T

            cols = pl.ds(pl.multiple_of(j * BLOCK, BLOCK), BLOCK)
            for arr in range(3):
                left = xb[pl.ds(group * 2, 2), arr // 2].reshape(ROWS, BLOCK)
                if arr == 0:
                    term = jnp.dot(left, wg[:, cols], preferred_element_type=F32)
                elif arr == 1:
                    term = jnp.dot(left, wu[:, cols], preferred_element_type=F32)
                else:
                    term = lax.dot_general(left, wd[cols, :], NT, preferred_element_type=F32)
                term = term.astype(BF)
                for a in range(4):
                    part[slot, a, :, 3 * arr : 3 * arr + 3] = term[:, 128 * a : 128 * a + 128].reshape(4, 3, 16, 128)
            for m in (0, 1, 16, 17):
                send(u, slot, m).start()

        @at_stage(8)
        def _(u, slot, i1, i2):
            s, j = group_and_block(u)
            for m in (18, 19, 14, 15):
                send(u, slot, m).wait()

            which = s // 3

            @pl.when(j == 0)
            def _():
                acc[which] = jnp.zeros((ROWS, BLOCK), F32)

            cols = pl.ds(pl.multiple_of(j * BLOCK, BLOCK), BLOCK)
            total = acc[which]
            for arr, weight in ((1, wg), (2, wu)):
                left = jnp.concatenate(
                    [full[u, a, :, 3 * arr : 3 * arr + 3].reshape(ROWS, 128) for a in range(4)], axis=1
                )
                total = total + lax.dot_general(left, weight[:, cols], NT, preferred_element_type=F32)
            acc[which] = total

            @pl.when(j == blocks - 1)
            def _():
                for k in (0, 1):
                    mine = jnp.logical_and(s == 0, core == k)

                    @pl.when(mine)
                    def _():
                        landed[col] = acc[which, HALF * k : HALF * (k + 1)].astype(BF)

                    @pl.when(jnp.logical_not(mine))
                    def _():
                        stage[s, k] = acc[which, HALF * k : HALF * (k + 1)].astype(BF)
                        term_copy(s, k).start()

            @pl.when(jnp.logical_and(s == GROUPS - 1, j < blocks - TAIL))
            def _():
                weight_grads(j)

    @pl.loop(blocks - TAIL, blocks)
    def _(j):
        weight_grads(j)

    total = landed[col].astype(F32)
    for pz, pk in partners:
        source = pz * 2 + pk
        pltpu.make_async_remote_copy(
            src_ref=stage.at[0, 0], dst_ref=landed.at[source], send_sem=is_sem.at[0, 0], recv_sem=ir_sem.at[source],
            device_id=(row, source), device_id_type=MESH,
        ).wait_recv()
        total = total + landed[source].astype(F32)
    out_ref[...] = total.astype(BF)

    for n in range(len(partners)):
        for c in shard_copies(n, col):
            c.wait_send()
    for s in range(GROUPS):
        for k in (0, 1):
            @pl.when(jnp.logical_not(jnp.logical_and(s == 0, core == k)))
            def _():
                term_copy(s, k).wait_send()


def local(layer_input, out_grad, gate_weight, up_weight, down_weight):
    depth, width = gate_weight.shape
    blocks = width // BLOCK
    units = GROUPS * blocks
    any_spec = pl.BlockSpec(memory_space=pl.ANY)
    tile = (16, 128)
    return pl.pallas_call(
        functools.partial(stream_kernel, 1.0 / (GROUPS * ROWS) ** 0.5),
        out_shape=(
            pltpu.VMEM((HALF, depth), BF),
            pltpu.VMEM((depth, width), BF),
            pltpu.VMEM((depth, width), BF),
            pltpu.VMEM((width, depth), BF),
        ),
        in_specs=[any_spec] * 5,
        out_specs=(pl.BlockSpec(memory_space=pltpu.VMEM),) * 4,
        scratch_shapes=[
            pltpu.VMEM((8, 2, HALF, depth), BF),
            pltpu.VMEM((GROUPS, depth, ROWS), BF),
            pltpu.VMEM((SLOTS, 4, 4, 9) + tile, BF),
            pltpu.VMEM((SLOTS, 2, 2, 9) + tile, BF),
            pltpu.VMEM((SLOTS, 2, 4, 9) + tile, BF),
            pltpu.VMEM((SLOTS, 9) + tile, BF),
            pltpu.VMEM((SLOTS, 2, 9) + tile, BF),
            pltpu.VMEM((units, 4, 4, 9) + tile, BF),
            pltpu.VMEM((2, ROWS, depth), F32),
            pltpu.VMEM((GROUPS, 2, HALF, depth), BF),
            pltpu.VMEM((8, HALF, depth), BF),
            pltpu.SemaphoreType.DMA((3, blocks)),
            pltpu.SemaphoreType.DMA((2,)),
            pltpu.SemaphoreType.DMA((7, 2)),
            pltpu.SemaphoreType.DMA((8, 2)),
            pltpu.SemaphoreType.DMA((SLOTS, 20)),
            pltpu.SemaphoreType.DMA((SLOTS, 20)),
            pltpu.SemaphoreType.DMA((GROUPS, 2)),
            pltpu.SemaphoreType.DMA((8,)),
        ],
        compiler_params=pltpu.CompilerParams(
            collective_id=0, has_side_effects=True, vmem_limit_bytes=48 * 2**20
        ),
        name="stream",
    )(layer_input, out_grad, gate_weight, up_weight, down_weight)


def solution(mesh):
    placed = (P("col", "row"), P("col", "row"), P("row", "col"), P("row", "col"), P("col", "row"))
    return jax.shard_map(
        local,
        mesh=mesh,
        in_specs=placed,
        out_specs=(P("col", "row"), P("row", "col"), P("row", "col"), P("col", "row")),
        check_vma=False,
    )
```

```python
import functools

import jax
import jax.numpy as jnp
from jax import lax
from jax.experimental import pallas as pl
from jax.experimental.pallas import tpu as pltpu
from jax.sharding import PartitionSpec as P

MESH = pl.DeviceIdType.MESH
BF = jnp.bfloat16
F32 = jnp.float32
NT = (((1,), (1,)), ((), ()))
TN = (((0,), (0,)), ((), ()))
GROUPS = 4
ROWS = 192
HALF = 96
SIDE = 4
BLOCK = 512
SLOTS = 14
TAIL = 2
STAGES = (0, 2, 4, 6, 8, 10, 12, 14, 16)


def stream_kernel(
    factor, x_hbm, dy_hbm, wg_hbm, wu_hbm, wd_hbm,
    out_ref, wg, wu, wd,
    xb, xt, part, r1, r2, r3, r4, full, acc, stage, landed,
    w_sem, x_sem, xs_sem, xr_sem, ssem, rsem, is_sem, ir_sem,
):
    blocks = wg.shape[1] // BLOCK
    units = GROUPS * blocks
    row = lax.axis_index("row")
    col = lax.axis_index("col")
    y, x = row // SIDE, lax.rem(row, SIDE)
    z, core = col // 2, lax.rem(col, 2)

    def add(a, n):
        return lax.rem(a + n, 4)

    def group_and_block(u):
        v = u - 2 * blocks
        s = jnp.where(v < 0, jnp.where(u < blocks, 0, 2), 1 + 2 * lax.rem(jnp.maximum(v, 0), 2))
        return s, jnp.where(v < 0, lax.rem(u, blocks), jnp.maximum(v, 0) // 2)

    def unit_of(n, j):
        return (j, 2 * blocks + 2 * j, blocks + j, 2 * blocks + 1 + 2 * j)[n]

    def weight_copies(j):
        cols = pl.ds(pl.multiple_of(j * BLOCK, BLOCK), BLOCK)
        return (
            pltpu.make_async_copy(wg_hbm.at[:, cols], wg.at[:, cols], w_sem.at[0, j]),
            pltpu.make_async_copy(wu_hbm.at[:, cols], wu.at[:, cols], w_sem.at[1, j]),
            pltpu.make_async_copy(wd_hbm.at[cols, :], wd.at[cols, :], w_sem.at[2, j]),
        )

    own = (
        pltpu.make_async_copy(x_hbm, xb.at[col, 0], x_sem.at[0]),
        pltpu.make_async_copy(dy_hbm, xb.at[col, 1], x_sem.at[1]),
    )
    for c in weight_copies(0) + own + weight_copies(1):
        c.start()

    partners = [(z, 1 - core)] + [(add(z, 4 - d), k) for d in (1, 2, 3) for k in (0, 1)]
    around = [(y, add(x, 1)), (y, add(x, 3)), (add(y, 1), x), (add(y, 3), x)]
    barrier = pltpu.get_barrier_semaphore()
    for pz, pk in partners:
        pl.semaphore_signal(barrier, inc=1, device_id=(row, pz * 2 + pk), device_id_type=MESH)
    for py, px in around:
        pl.semaphore_signal(barrier, inc=1, device_id=(py * SIDE + px, col), device_id_type=MESH)
    pl.semaphore_wait(barrier, len(partners) + len(around))

    def shard_copies(n, source):
        pz, pk = partners[n]
        return [
            pltpu.make_async_remote_copy(
                src_ref=ref, dst_ref=xb.at[source, h], send_sem=xs_sem.at[n, h], recv_sem=xr_sem.at[source, h],
                device_id=(row, pz * 2 + pk), device_id_type=MESH,
            )
            for h, ref in enumerate((x_hbm, dy_hbm))
        ]

    for n in range(len(partners)):
        for c in shard_copies(n, col):
            c.start()
    for c in own:
        c.wait()
    for c in shard_copies(0, z * 2 + 1 - core):
        c.wait_recv()

    def term_copy(s, k):
        return pltpu.make_async_remote_copy(
            src_ref=stage.at[s, k], dst_ref=landed.at[col], send_sem=is_sem.at[s, k], recv_sem=ir_sem.at[col],
            device_id=(row, add(z, s) * 2 + k), device_id_type=MESH,
        )

    def weight_grads(j):
        cols = pl.ds(pl.multiple_of(j * BLOCK, BLOCK), BLOCK)

        def gathered(arr, n):
            return jnp.concatenate(
                [full[unit_of(n, j), a, :, 3 * arr : 3 * arr + 3].reshape(ROWS, 128) for a in range(4)],
                axis=1,
            )

        for arr, grad in ((1, wg), (2, wu)):
            right = jnp.concatenate([gathered(arr, n) for n in range(GROUPS)], axis=0)
            total = jnp.dot(xt[...], right, preferred_element_type=F32)
            grad[:, cols] = (total * factor).astype(BF)
        hidden = jnp.concatenate([gathered(0, n) for n in range(GROUPS)], axis=0)
        right = jnp.concatenate(
            [xb[pl.ds(add(z, n) * 2, 2), 1].reshape(ROWS, BLOCK) for n in range(GROUPS)], axis=0
        )
        wd[cols, :] = (lax.dot_general(hidden, right, TN, preferred_element_type=F32) * factor).astype(BF)

    @pl.loop(0, units + STAGES[-1])
    def _(t):
        def send(u, slot, m):
            even = lax.rem(u, 2) == 0
            i1, i2 = jnp.where(even, x, y), jnp.where(even, y, x)

            def device(d1, d2):
                a, b = add(i1, d1), add(i2, d2)
                return (jnp.where(even, b, a) * SIDE + jnp.where(even, a, b), col)

            up1, down1, up2, down2 = device(1, 0), device(3, 0), device(0, 1), device(0, 3)
            n1, p1, f1 = add(i1, 1), add(i1, 3), add(i1, 2)
            n2, p2, f2 = add(i2, 1), add(i2, 3), add(i2, 2)
            src, dst, target = {
                0: (lambda: part.at[slot, f1, pl.ds(0, 2)], lambda: r1.at[slot, 0], up1),
                1: (lambda: part.at[slot, f1, pl.ds(2, 2)], lambda: r1.at[slot, 1], down1),
                2: (lambda: part.at[slot, n1, pl.ds(0, 2)], lambda: r2.at[slot, 0, pl.ds(0, 2)], up1),
                3: (lambda: part.at[slot, p1, pl.ds(2, 2)], lambda: r2.at[slot, 1, pl.ds(2, 2)], down1),
                4: (lambda: part.at[slot, i1, f2, pl.ds(0, 5)], lambda: r3.at[slot, pl.ds(0, 5)], up2),
                5: (lambda: part.at[slot, i1, f2, pl.ds(5, 4)], lambda: r3.at[slot, pl.ds(5, 4)], down2),
                6: (lambda: part.at[slot, i1, n2], lambda: r4.at[slot, 0], up2),
                7: (lambda: part.at[slot, i1, p2], lambda: r4.at[slot, 1], down2),
                8: (lambda: full.at[u, i1, i2], lambda: full.at[u, i1, i2], up2),
                9: (lambda: full.at[u, i1, i2], lambda: full.at[u, i1, i2], down2),
                10: (lambda: full.at[u, i1, p2, pl.ds(0, 5)], lambda: full.at[u, i1, p2, pl.ds(0, 5)], up2),
                11: (lambda: full.at[u, i1, n2, pl.ds(5, 4)], lambda: full.at[u, i1, n2, pl.ds(5, 4)], down2),
                12: (lambda: full.at[u, i1, pl.ds(0, 2)], lambda: full.at[u, i1, pl.ds(0, 2)], up1),
                13: (lambda: full.at[u, i1, pl.ds(2, 2)], lambda: full.at[u, i1, pl.ds(2, 2)], down1),
                14: (lambda: full.at[u, p1, pl.ds(0, 2)], lambda: full.at[u, p1, pl.ds(0, 2)], up1),
                15: (lambda: full.at[u, n1, pl.ds(2, 2)], lambda: full.at[u, n1, pl.ds(2, 2)], down1),
                16: (lambda: part.at[slot, n1, pl.ds(2, 2)], lambda: r2.at[slot, 0, pl.ds(2, 2)], up1),
                17: (lambda: part.at[slot, p1, pl.ds(0, 2)], lambda: r2.at[slot, 1, pl.ds(0, 2)], down1),
                18: (lambda: full.at[u, i1, pl.ds(2, 2)], lambda: full.at[u, i1, pl.ds(2, 2)], up1),
                19: (lambda: full.at[u, i1, pl.ds(0, 2)], lambda: full.at[u, i1, pl.ds(0, 2)], down1),
            }[m]
            return pltpu.make_async_remote_copy(
                src_ref=src(), dst_ref=dst(), send_sem=ssem.at[slot, m], recv_sem=rsem.at[slot, m],
                device_id=target, device_id_type=MESH,
            )

        def at_stage(k):
            u = t - STAGES[k]

            def run(body):
                @pl.when(jnp.logical_and(u >= 0, u < units))
                def _():
                    even = lax.rem(u, 2) == 0
                    i1, i2 = jnp.where(even, x, y), jnp.where(even, y, x)
                    body(u, lax.rem(u, SLOTS), i1, i2)
            return run

        @at_stage(7)
        def _(u, slot, i1, i2):
            send(u, slot, 12).wait()
            send(u, slot, 14).start()
            send(u, slot, 13).wait()
            send(u, slot, 15).start()

        @at_stage(6)
        def _(u, slot, i1, i2):
            send(u, slot, 10).wait()
            send(u, slot, 11).wait()
            for m in (12, 13, 18, 19):
                send(u, slot, m).start()

        @at_stage(5)
        def _(u, slot, i1, i2):
            send(u, slot, 8).wait()
            send(u, slot, 10).start()
            send(u, slot, 9).wait()
            send(u, slot, 11).start()

        @at_stage(4)
        def _(u, slot, i1, i2):
            send(u, slot, 6).wait()
            send(u, slot, 7).wait()
            total = (
                part[slot, i1, i2].astype(F32) + r4[slot, 0].astype(F32) + r4[slot, 1].astype(F32)
            )
            gate, up, hidden_grad = total[0:3], total[3:6], total[6:9]
            sigma = 1.0 / (1.0 + jnp.exp(-gate))
            swish = gate * sigma
            full[u, i1, i2, 0:3] = (swish * up).astype(BF)
            full[u, i1, i2, 3:6] = (hidden_grad * up * sigma * (1.0 + gate * (1.0 - sigma))).astype(BF)
            full[u, i1, i2, 6:9] = (hidden_grad * swish).astype(BF)
            send(u, slot, 8).start()
            send(u, slot, 9).start()

        @at_stage(3)
        def _(u, slot, i1, i2):
            send(u, slot, 4).wait()
            part[slot, i1, add(i2, 1), 0:5] = (part[slot, i1, add(i2, 1), 0:5].astype(F32) + r3[slot, 0:5].astype(F32)).astype(BF)
            send(u, slot, 6).start()
            send(u, slot, 5).wait()
            part[slot, i1, add(i2, 3), 5:9] = (part[slot, i1, add(i2, 3), 5:9].astype(F32) + r3[slot, 5:9].astype(F32)).astype(BF)
            send(u, slot, 7).start()

        @at_stage(2)
        def _(u, slot, i1, i2):
            for m in (16, 17, 2, 3):
                send(u, slot, m).wait()
            part[slot, i1] = (
                part[slot, i1].astype(F32) + r2[slot, 0].astype(F32) + r2[slot, 1].astype(F32)
            ).astype(BF)
            send(u, slot, 4).start()
            send(u, slot, 5).start()

        @at_stage(1)
        def _(u, slot, i1, i2):
            send(u, slot, 0).wait()
            part[slot, add(i1, 1), 0:2] = (part[slot, add(i1, 1), 0:2].astype(F32) + r1[slot, 0].astype(F32)).astype(BF)
            send(u, slot, 2).start()
            send(u, slot, 1).wait()
            part[slot, add(i1, 3), 2:4] = (part[slot, add(i1, 3), 2:4].astype(F32) + r1[slot, 1].astype(F32)).astype(BF)
            send(u, slot, 3).start()

        @at_stage(0)
        def _(u, slot, i1, i2):
            s, j = group_and_block(u)
            group = add(z, s)

            @pl.when(s == 0)
            def _():
                for c in weight_copies(j):
                    c.wait()

                @pl.when(j + 2 < blocks)
                def _():
                    for c in weight_copies(j + 2):
                        c.start()

            @pl.when(jnp.logical_and(s > 0, j == 0))
            def _():
                for k in (0, 1):
                    for c in shard_copies(1, group * 2 + k):
                        c.wait_recv()

            @pl.when(jnp.logical_and(s == GROUPS - 1, j == 1))
            def _():
                xt[...] = jnp.concatenate(
                    [xb[pl.ds(add(z, n) * 2, 2), 0].reshape(ROWS, BLOCK) for n in range(GROUPS)], axis=0
                ).T

            cols = pl.ds(pl.multiple_of(j * BLOCK, BLOCK), BLOCK)
            for arr in range(3):
                left = xb[pl.ds(group * 2, 2), arr // 2].reshape(ROWS, BLOCK)
                if arr == 0:
                    term = jnp.dot(left, wg[:, cols], preferred_element_type=F32)
                elif arr == 1:
                    term = jnp.dot(left, wu[:, cols], preferred_element_type=F32)
                else:
                    term = lax.dot_general(left, wd[cols, :], NT, preferred_element_type=F32)
                term = term.astype(BF)
                for a in range(4):
                    part[slot, a, :, 3 * arr : 3 * arr + 3] = term[:, 128 * a : 128 * a + 128].reshape(4, 3, 16, 128)
            for m in (0, 1, 16, 17):
                send(u, slot, m).start()

        @at_stage(8)
        def _(u, slot, i1, i2):
            s, j = group_and_block(u)
            for m in (18, 19, 14, 15):
                send(u, slot, m).wait()

            which = s // 3

            @pl.when(j == 0)
            def _():
                acc[which] = jnp.zeros((ROWS, BLOCK), F32)

            cols = pl.ds(pl.multiple_of(j * BLOCK, BLOCK), BLOCK)
            total = acc[which]
            for arr, weight in ((1, wg), (2, wu)):
                left = jnp.concatenate(
                    [full[u, a, :, 3 * arr : 3 * arr + 3].reshape(ROWS, 128) for a in range(4)], axis=1
                )
                total = total + lax.dot_general(left, weight[:, cols], NT, preferred_element_type=F32)
            acc[which] = total

            @pl.when(j == blocks - 1)
            def _():
                for k in (0, 1):
                    mine = jnp.logical_and(s == 0, core == k)

                    @pl.when(mine)
                    def _():
                        landed[col] = acc[which, HALF * k : HALF * (k + 1)].astype(BF)

                    @pl.when(jnp.logical_not(mine))
                    def _():
                        stage[s, k] = acc[which, HALF * k : HALF * (k + 1)].astype(BF)
                        term_copy(s, k).start()

            @pl.when(jnp.logical_and(s == GROUPS - 1, j < blocks - TAIL))
            def _():
                weight_grads(j)

    @pl.loop(blocks - TAIL, blocks)
    def _(j):
        weight_grads(j)

    total = landed[col].astype(F32)
    for pz, pk in partners:
        source = pz * 2 + pk
        pltpu.make_async_remote_copy(
            src_ref=stage.at[0, 0], dst_ref=landed.at[source], send_sem=is_sem.at[0, 0], recv_sem=ir_sem.at[source],
            device_id=(row, source), device_id_type=MESH,
        ).wait_recv()
        total = total + landed[source].astype(F32)
    out_ref[...] = total.astype(BF)

    for n in range(len(partners)):
        for c in shard_copies(n, col):
            c.wait_send()
    for s in range(GROUPS):
        for k in (0, 1):
            @pl.when(jnp.logical_not(jnp.logical_and(s == 0, core == k)))
            def _():
                term_copy(s, k).wait_send()


def local(layer_input, out_grad, gate_weight, up_weight, down_weight):
    depth, width = gate_weight.shape
    blocks = width // BLOCK
    units = GROUPS * blocks
    any_spec = pl.BlockSpec(memory_space=pl.ANY)
    tile = (16, 128)
    return pl.pallas_call(
        functools.partial(stream_kernel, 1.0 / (GROUPS * ROWS) ** 0.5),
        out_shape=(
            pltpu.VMEM((HALF, depth), BF),
            pltpu.VMEM((depth, width), BF),
            pltpu.VMEM((depth, width), BF),
            pltpu.VMEM((width, depth), BF),
        ),
        in_specs=[any_spec] * 5,
        out_specs=(pl.BlockSpec(memory_space=pltpu.VMEM),) * 4,
        scratch_shapes=[
            pltpu.VMEM((8, 2, HALF, depth), BF),
            pltpu.VMEM((depth, GROUPS * ROWS), BF),
            pltpu.VMEM((SLOTS, 4, 4, 9) + tile, BF),
            pltpu.VMEM((SLOTS, 2, 2, 9) + tile, BF),
            pltpu.VMEM((SLOTS, 2, 4, 9) + tile, BF),
            pltpu.VMEM((SLOTS, 9) + tile, BF),
            pltpu.VMEM((SLOTS, 2, 9) + tile, BF),
            pltpu.VMEM((units, 4, 4, 9) + tile, BF),
            pltpu.VMEM((2, ROWS, depth), F32),
            pltpu.VMEM((GROUPS, 2, HALF, depth), BF),
            pltpu.VMEM((8, HALF, depth), BF),
            pltpu.SemaphoreType.DMA((3, blocks)),
            pltpu.SemaphoreType.DMA((2,)),
            pltpu.SemaphoreType.DMA((7, 2)),
            pltpu.SemaphoreType.DMA((8, 2)),
            pltpu.SemaphoreType.DMA((SLOTS, 20)),
            pltpu.SemaphoreType.DMA((SLOTS, 20)),
            pltpu.SemaphoreType.DMA((GROUPS, 2)),
            pltpu.SemaphoreType.DMA((8,)),
        ],
        compiler_params=pltpu.CompilerParams(
            collective_id=0, has_side_effects=True, vmem_limit_bytes=48 * 2**20
        ),
        name="stream",
    )(layer_input, out_grad, gate_weight, up_weight, down_weight)


def solution(mesh):
    placed = (P("col", "row"), P("col", "row"), P("row", "col"), P("row", "col"), P("col", "row"))
    return jax.shard_map(
        local,
        mesh=mesh,
        in_specs=placed,
        out_specs=(P("col", "row"), P("row", "col"), P("row", "col"), P("col", "row")),
        check_vma=False,
    )
```
